256 devices in a mesh: walk: 16 (over x, z_hi), pt: 16 (over y, z_lo, core).
Axes of the slice: x: 4, y: 4, z: 8 (z_hi: 4, z_lo: 2; z = z_hi * 2 + z_lo), core: 2. Of those that a mesh axis runs over, the one named last changes fastest.
Arguments:
- bra_orbitals: bfloat16 [16, 1536, 160], P('walk'), may hold values from -6 to 6
- ket_orbitals: bfloat16 [16, 1536, 160], P('walk'), may hold values from -6 to 6
- collocation: bfloat16 [12288, 1536], P('pt'), may hold values from -0.15625 to 0.15625
- kernel: bfloat16 [12288, 12288], P('pt', 'walk'), as said below
- walker_weight: float32 [16], P('walk'), may hold values from 0.3 to 3
- walker_group: int32 [16], P('walk'), may hold values from 0 to 19
- group_occupied: int32 [20], replicated, may hold values from 80 to 160, as said below
Outputs:
- gradient: float32 [12288, 1536], P('pt', 'walk')
The draws below stay inside these ranges and needn't reach their ends.
Inputs may be any that keep to these rules, and one draw needn't show every extreme that they name: kernel is symmetric. `group_occupied`: some group has exactly 160 occupied orbitals.
All inputs are finite; a program needn't handle non-finite values.
Results may differ from the reference program's by a relative error of at most 0.0064.
Values may be sent and summed in bfloat16 or wider, within the bound.
A program may use at most 128 MiB of HBM per device.

```python
import math
import jax
import jax.numpy as jnp
from jax import lax

M = 1536
NOCC = 160
P_SIZE = 12288
GROUPS = 20
WALKERS = 16
N_PT = 16


def draw_kernel(key, part):
    values = jax.random.normal(key, (P_SIZE, P_SIZE), jnp.float32)
    factor = 1.0 / math.sqrt(2.0 * P_SIZE * NOCC)
    return ((values + values.T) * factor).astype(jnp.bfloat16)


def draw_group_occupied(key, part):
    counts = jax.random.randint(key, (GROUPS,), NOCC // 2, NOCC + 1, dtype=jnp.int32)
    chosen = jax.random.randint(jax.random.fold_in(key, 7), (), 0, GROUPS, dtype=jnp.int32)
    positions = jnp.arange(GROUPS, dtype=jnp.int32)
    return jnp.where(positions == chosen, NOCC, counts).astype(jnp.int32)


def with_ends(values, stream_key, smallest, top_value):
    longest = values.shape.index(max(values.shape))
    spots = []
    for shift in (0, 1):
        where = [jax.random.randint(jax.random.fold_in(stream_key, axis), (), 0, length) for axis, length in enumerate(values.shape)]
        where[longest] = (where[longest] + shift) % values.shape[longest]
        spots.append(tuple(where))
    return values.at[spots[0]].set(smallest).at[spots[1]].set(top_value)


def shard_levels(stream_key, shape, cuts, least, largest):
    def one(dim, blocks):
        heights = jax.random.uniform(jax.random.fold_in(jax.random.fold_in(stream_key, 6), dim), (blocks,), jnp.float32, least / len(cuts), largest / len(cuts))
        return jnp.repeat(jnp.exp(heights), shape[dim] // blocks).reshape((-1,) + (1,) * (len(shape) - dim - 1))

    loudness = one(*cuts[0])
    for cut in cuts[1:]:
        loudness = loudness * one(*cut)
    return loudness


def bell_draw(key, shape, spread, bound, shards=(), kind=jnp.bfloat16):
    values = spread * jax.random.normal(key, shape, jnp.float32)
    if shards:
        values = values * shard_levels(key, shape, shards, -0.22, 0.18)
    return jnp.clip(values, -bound, bound).astype(kind)


def setup_inputs(seed: int = 0) -> dict:
    streams_of = jax.random.split(jax.random.key(seed), 8)
    bra_orbitals = bell_draw(streams_of[0], (WALKERS, M, NOCC), 1.0, 6.0, ((0, 16),))
    ket_orbitals = bell_draw(streams_of[1], (WALKERS, M, NOCC), 1.0, 6.0, ((0, 16),))
    collocation = bell_draw(streams_of[2], (P_SIZE, M), M ** -0.5, 0.15625, ((0, 16),))
    kernel = draw_kernel(jax.random.fold_in(streams_of[7], 71), 0)
    walker_weight = jnp.clip(jnp.exp(math.log(3.0) - 2.3025851 * jax.random.uniform(streams_of[4], (WALKERS,), jnp.float32) ** shard_levels(streams_of[4], (WALKERS,), ((0, 16),), -0.2, 0.2)), 0.3, 3.0)
    walker_group = with_ends(jax.random.randint(streams_of[5], (WALKERS,), 0, GROUPS), jax.random.fold_in(streams_of[5], 1), 0, GROUPS - 1).astype(jnp.int32)
    group_occupied = draw_group_occupied(jax.random.fold_in(streams_of[7], 71), 0)
    return {"bra_orbitals": bra_orbitals, "ket_orbitals": ket_orbitals, "collocation": collocation, "kernel": kernel, "walker_weight": walker_weight, "walker_group": walker_group, "group_occupied": group_occupied}


def reference(bra_orbitals, ket_orbitals, collocation, kernel, walker_weight, walker_group, group_occupied):
    occupied = group_occupied[walker_group]
    masks = (jnp.arange(NOCC, dtype=jnp.int32)[None, :] < occupied[:, None]).astype(jnp.bfloat16)
    shares = walker_weight / jnp.sum(walker_weight)
    block_rows = P_SIZE // N_PT

    def one_walker(totals, inputs):
        bra_raw, ket_raw, mask_row, share_one = inputs
        left_bra = bra_raw * mask_row[None, :]
        right_ket = ket_raw * mask_row[None, :]
        lefts = jnp.dot(collocation, left_bra, preferred_element_type=jnp.float32).astype(jnp.bfloat16)
        rights = jnp.dot(collocation, right_ket, preferred_element_type=jnp.float32).astype(jnp.bfloat16)

        def block(begin):
            left_rows = lax.dynamic_slice_in_dim(lefts, begin, block_rows, 0)
            right_rows = lax.dynamic_slice_in_dim(rights, begin, block_rows, 0)
            kernel_rows = lax.dynamic_slice_in_dim(kernel, begin, block_rows, 0).astype(jnp.float32)
            green_t = jnp.dot(right_rows, lefts.T, preferred_element_type=jnp.float32)
            green = jnp.dot(left_rows, rights.T, preferred_element_type=jnp.float32)
            hadamard_t = (kernel_rows * green_t).astype(jnp.bfloat16)
            hadamard = (kernel_rows * green).astype(jnp.bfloat16)
            grad_left = (2.0 * jnp.dot(hadamard_t, rights, preferred_element_type=jnp.float32)).astype(jnp.bfloat16)
            grad_right = (2.0 * jnp.dot(hadamard, lefts, preferred_element_type=jnp.float32)).astype(jnp.bfloat16)
            return jnp.dot(grad_left, left_bra.T, preferred_element_type=jnp.float32) + jnp.dot(grad_right, right_ket.T, preferred_element_type=jnp.float32)

        starts = jnp.arange(N_PT, dtype=jnp.int32) * block_rows
        term = lax.map(block, starts).reshape(P_SIZE, M)
        return totals + share_one * term, None

    start_total = jnp.zeros((P_SIZE, M), jnp.float32)
    result, unused = lax.scan(one_walker, start_total, (bra_orbitals, ket_orbitals, masks, shares))
    return result
```

```python
import jax
import jax.numpy as jnp
from jax import lax
from jax.experimental import pallas as pl
from jax.experimental.pallas import tpu as pltpu
from jax.sharding import PartitionSpec as P

MESH = pl.DeviceIdType.MESH
F32 = jnp.float32
BF16 = jnp.bfloat16
NT = (((1,), (1,)), ((), ()))
TILE = 256


def kernel(
    weight, group, occupied, bra, ket, coll, kern, out,
    vt, lta, lb, kb, grad, wz, wx, chunk, po, xa, xb, xl, xr, own, tz, zs, zt, za, zb, zl_, zr_,
    vs, vr, ls, lr, ks_, kr, ws, wr, os_, or_, loc,
):
    wi, pi = lax.axis_index("walk"), lax.axis_index("pt")
    x, zh, y, s = wi // 4, wi % 4, pi // 4, pi % 4
    zl, c = s // 2, s % 2
    occ, mm, rows = bra.shape[0], bra.shape[1], coll.shape[0]
    half = occ // 2
    krows = rows // 2

    def dev(x_, zh_, y_, s_):
        return {"walk": x_ * 4 + zh_, "pt": y_ * 4 + s_}

    xp, xm, x2 = (dev((x + d) % 4, zh, y, s) for d in (1, 3, 2))
    zp, zm, z2 = (dev(x, (zh + d) % 4, y, s) for d in (1, 3, 2))
    yp, ym = (dev(x, zh, (y + d) % 4, s) for d in (1, 3))
    oz = (zh * 2 + zl + 7 + 2 * zl) % 8
    outer = dev(x, oz // 2, y, (oz % 2) * 2 + c)
    inner = dev(x, zh, y, (1 - zl) * 2 + c)
    mate = dev(x, zh, y, zl * 2 + 1 - c)
    ro, ri = 3 - 2 * zl, 1 + 2 * zl
    slots = (0, ro, ri, 2)
    hf = pl.ds(pl.multiple_of(half * (1 - zl), 16), half)
    ho = pl.ds(pl.multiple_of(half * zl, 16), half)
    home = s == zh
    lead = c == zh % 2
    other = jnp.logical_and(lead, s != zh)

    barrier = pltpu.get_barrier_semaphore()
    peers = (xp, xm, x2, zp, zm, z2, yp, ym, outer, inner, mate)
    for peer in peers:
        pl.semaphore_signal(barrier, inc=1, device_id=peer, device_id_type=MESH)

    sent = []

    def copy(src, dst, send, recv, to):
        return pltpu.make_async_remote_copy(
            src_ref=src, dst_ref=dst, send_sem=send, recv_sem=recv, device_id=to,
            device_id_type=MESH,
        )

    def send(make, cond=None):
        make().start()
        sent.append((make, cond))

    live = lax.broadcasted_iota(jnp.int32, (occ, mm), 0) < occupied[group[0]]
    vt[0, 0] = jnp.where(live, bra[...], jnp.zeros_like(bra[...]))
    vt[0, 1] = jnp.where(live, ket[...], jnp.zeros_like(ket[...]))
    wz[0] = jnp.full(wz.shape[1:], weight[0], F32)
    local = pltpu.make_async_copy(kern, kb.at[0], loc)
    local.start()
    pl.semaphore_wait(barrier, len(peers))

    def kpart(i, slot, n):
        return kb.at[slot, pl.ds(n * krows, krows)]

    def kcopy(i, slot, n, to, src=None):
        src = kern.at[pl.ds(n * krows, krows)] if src is None else src
        return copy(src, kpart(i, slot, n), ks_.at[i], kr.at[i], to)

    def vcopy(i, src_slot, slot, side, part, to):
        return copy(
            vt.at[src_slot, side, part], vt.at[slot, side, part], vs.at[i], vr.at[i], to
        )

    send(lambda: vcopy(0, 0, ri, c, hf, outer))
    send(lambda: kcopy(0, 3, 0, xp))
    send(lambda: kcopy(1, 1, 1, xm))
    send(lambda: vcopy(1, 0, ri, c, ho, outer))
    send(lambda: kcopy(2, 3, 1, xp))
    send(lambda: kcopy(3, 1, 0, xm))
    for d, to in ((1, zp), (2, z2), (3, zm)):
        send(lambda d=d, to=to: copy(wz.at[0], wz.at[4 - d], ws.at[d - 1], wr.at[d - 1], to))

    def vwait(i, slot, side, part, to):
        vcopy(i, slot, slot, side, part, to).wait_recv()

    def s1a():
        vwait(0, ro, c, ho, outer)
        send(lambda: vcopy(2, ro, ro, c, ho, inner))
        send(lambda: vcopy(6, ro, ro, c, ho, mate))

    def s1b():
        vwait(1, ro, c, hf, outer)
        send(lambda: vcopy(3, ro, ro, c, hf, inner))
        send(lambda: vcopy(7, ro, ro, c, hf, mate))

    def s2a():
        vwait(2, ri, c, hf, inner)
        send(lambda: vcopy(4, ri, 2, c, hf, outer))
        send(lambda: vcopy(8, ri, ri, c, hf, mate))

    def s2b():
        vwait(3, ri, c, ho, inner)
        send(lambda: vcopy(9, ri, ri, c, ho, mate))

    def s3():
        vwait(4, 2, c, ho, outer)
        send(lambda: vcopy(5, 2, 2, c, ho, inner))
        send(lambda: vcopy(10, 2, 2, c, ho, mate))

    def s4():
        vwait(5, 2, c, hf, inner)
        send(lambda: vcopy(11, 2, 2, c, hf, mate))

    def vmate(kk):
        slot = slots[kk]
        first, second = ((ho, hf), (hf, ho), (ho, hf))[kk - 1]
        vwait(4 + 2 * kk, slot, 1 - c, first, mate)
        vwait(5 + 2 * kk, slot, 1 - c, second, mate)

    def krelay():
        kcopy(0, 3, 0, xp).wait_recv()
        send(lambda: kcopy(4, 2, 0, xp, kpart(0, 3, 0)))
        kcopy(1, 1, 1, xm).wait_recv()
        send(lambda: kcopy(5, 2, 1, xm, kpart(1, 1, 1)))

    def lcopy(i, src, dst, slot, to):
        return copy(src, dst, ls.at[i, slot], lr.at[i, slot], to)

    def spread(kk, cond):
        slot = slots[kk]
        send(lambda: lcopy(1, lta.at[0, slot], lta.at[3, slot], slot, yp), cond)
        send(lambda: lcopy(2, lta.at[0, slot], lta.at[1, slot], slot, ym), cond)
        send(lambda: lcopy(5, lta.at[0, slot], lta.at[0, slot], slot, mate), cond)

    def spread_home(kk):
        @pl.when(home)
        def _():
            slot = slots[kk]
            send(lambda: lcopy(0, lta.at[0, slot], lta.at[0, slot], slot, inner), home)
            spread(kk, home)

    def h1(kk):
        @pl.when(other)
        def _():
            slot = slots[kk]
            here = lta.at[0, slot]
            lcopy(0, here, here, slot, inner).wait_recv()
            spread(kk, other)

    def yrelay(kk, cond):
        @pl.when(cond)
        def _():
            slot = slots[kk]
            low, high = lta.at[3, slot], lta.at[1, slot]
            lcopy(1, low, low, slot, yp).wait_recv()
            send(lambda: lcopy(3, lta.at[3, slot, 0], lta.at[2, slot, 0], slot, yp), cond)
            send(lambda: lcopy(8, lta.at[3, slot], lta.at[3, slot], slot, mate), cond)
            lcopy(2, high, high, slot, ym).wait_recv()
            send(lambda: lcopy(4, lta.at[1, slot, 1], lta.at[2, slot, 1], slot, ym), cond)
            send(lambda: lcopy(6, lta.at[1, slot], lta.at[1, slot], slot, mate), cond)

    def r2(kk):
        @pl.when(lead)
        def _():
            slot = slots[kk]
            one, two = lta.at[2, slot, 0], lta.at[2, slot, 1]
            lcopy(3, one, one, slot, yp).wait_recv()
            lcopy(4, two, two, slot, ym).wait_recv()
            send(lambda: lcopy(7, lta.at[2, slot], lta.at[2, slot], slot, mate), lead)

    def weights():
        for d, to in ((1, zp), (2, z2), (3, zm)):
            copy(wz.at[4 - d], wz.at[4 - d], ws.at[d - 1], wr.at[d - 1], to).wait_recv()
        wx[0] = wz[0] + wz[1] + wz[2] + wz[3]
        for d, to in ((1, xp), (2, x2), (3, xm)):
            send(lambda d=d, to=to: copy(wx.at[0], wx.at[4 - d], ws.at[d + 2], wr.at[d + 2], to))

    relays = {
        1: [s1a, lambda: yrelay(0, home), krelay, s1b, s2a, lambda: h1(0), lambda: vmate(1)],
        2: [s2b, s3, lambda: yrelay(0, other), lambda: vmate(2)],
        3: [lambda: yrelay(1, home), lambda: h1(1), lambda: r2(0), weights, local.wait],
        4: [lambda: (kcopy(2, 3, 1, xp).wait_recv(), kcopy(3, 1, 0, xm).wait_recv())],
        5: [s4, lambda: yrelay(2, home), lambda: yrelay(1, other), lambda: h1(2), lambda: vmate(3)],
        6: [lambda: r2(1)],
        8: [lambda: yrelay(2, other), lambda: h1(3)],
        9: [lambda: r2(2)],
        11: [lambda: yrelay(3, home)],
        13: [
            lambda: kcopy(4, 2, 0, xp).wait_recv(),
            lambda: kcopy(5, 2, 1, xm).wait_recv(),
            lambda: yrelay(3, other),
        ],
        16: [lambda: r2(3)],
    }

    def tri(n):
        return (n * (n + 1) // 2) % 4

    def project(kk):
        slot = (tri(kk) * ro) % 4
        both = vt[slot].reshape(2 * occ, mm)
        pts = lax.dot_general(both, coll[...], NT, preferred_element_type=F32).astype(BF16)
        for side in range(2):
            lb[slot, side] = pts[side * occ : (side + 1) * occ].T

        @pl.when(home)
        def _():
            lta[0, slot] = pts.reshape(2, occ, rows)

    def unit(i):
        f, g = i // 9, i // 12
        kk = (1 - f) * (i // 3) + (f - g) * (i - 9) + g * 3
        jj = (1 - f) * (i % 3) + (f - g) * 3 + g * (i - 12)
        slot = (tri(kk) * ro) % 4
        j = tri(jj)
        yr = (x + j - y + 4) % 4

        @pl.when(jnp.logical_not(lead))
        def _():
            here = lta.at[yr, slot]
            lcopy(5 + yr, here, here, slot, mate).wait_recv()

        total = [None, None]
        for q in range(rows // TILE):
            cols = pl.ds(q * TILE, TILE)
            kq = kb[j, :, cols].astype(F32)
            for side in range(2):
                green = jnp.dot(
                    lb[slot, side], lta[yr, slot, 1 - side, :, cols], preferred_element_type=F32
                )
                had = (kq * green).astype(BF16)
                more = lax.dot_general(
                    had, lta[yr, slot, side, :, cols], NT, preferred_element_type=F32
                )
                total[side] = more if total[side] is None else total[side] + more
        for side in range(2):
            grad[slot, side] += total[1 - side]

    for slot in range(4):
        for side in range(2):
            grad[slot, side] = jnp.zeros(grad.shape[2:], F32)

    def step(t, carry):
        for at, todo in relays.items():

            @pl.when(t == at)
            def _():
                for one in todo:
                    one()

        proj = jnp.logical_or(t < 3, t == 5)

        @pl.when(proj)
        def _():
            project(t - 2 * (t // 5))

        for at, kk in ((0, 0), (1, 1), (2, 2), (5, 3)):

            @pl.when(t == at)
            def _():
                spread_home(kk)

        @pl.when(jnp.logical_not(proj))
        def _():
            unit(t - 3 - t // 6 + t // 12 + t // 18)

        return carry

    lax.fori_loop(0, 20, step, 0)

    for d, to in ((1, xp), (2, x2), (3, xm)):
        copy(wx.at[4 - d], wx.at[4 - d], ws.at[d + 2], wr.at[d + 2], to).wait_recv()
    whole = wx[0] + wx[1] + wx[2] + wx[3]

    def scale(i, carry):
        slot, side = i // 2, i % 2
        share = (2.0 * wz[slot] / whole)[0:1, :occ]
        lb[slot, side] = (grad[slot, side] * share).astype(BF16)
        return carry

    lax.fori_loop(0, 8, scale, 0)

    hrows = rows // 2
    qrows = rows // 4
    width = mm // 4
    piece = width // 4

    def xcopy(i, h, src, dst, to):
        return copy(src, dst, os_.at[i, h], or_.at[i, h], to)

    def acopy(h):
        return (
            xcopy(0, h, po.at[h, 0, pl.ds(0, qrows)], xa.at[h], xp),
            xcopy(1, h, po.at[h, 0, pl.ds(qrows, qrows)], xb.at[h], xm),
        )

    def bcopy(h):
        return xcopy(2, h, po.at[h, 1], xl.at[h], xp), xcopy(3, h, po.at[h, 2], xr.at[h], xm)

    def tail(n, carry):
        h, ty = n % 2, n // 2
        d = (2 - tri(ty) + 4) % 4
        cols = pl.ds(pl.multiple_of(((x + d) % 4) * width, 128), width)
        part = pl.ds(pl.multiple_of(h * hrows, 16), hrows)
        acc = None
        for slot in range(4):
            for side in range(2):
                term = jnp.dot(
                    lb[slot, side, part], vt[slot, side, :, cols], preferred_element_type=F32
                )
                acc = term if acc is None else acc + term
        chunk[...] = acc

        @pl.when(ty == 0)
        def _():
            po[h, 0] = chunk[...].astype(BF16)
            for one in acopy(h):
                one.start()

        @pl.when(ty == 1)
        def _():
            acopy(h)[0].wait_recv()
            po[h, 1, :qrows] = (chunk[:qrows] + xa[h].astype(F32)).astype(BF16)
            po[h, 1, qrows:] = chunk[qrows:].astype(BF16)
            bcopy(h)[0].start()

        @pl.when(ty == 2)
        def _():
            acopy(h)[1].wait_recv()
            po[h, 2, :qrows] = chunk[:qrows].astype(BF16)
            po[h, 2, qrows:] = (chunk[qrows:] + xb[h].astype(F32)).astype(BF16)
            bcopy(h)[1].start()

        @pl.when(ty == 3)
        def _():
            own[h] = chunk[...]

        return carry

    lax.fori_loop(0, 8, tail, 0)

    low = piece // 2

    def zrows(d, n, size):
        return pl.ds(pl.multiple_of(((zh + d) % 4) * piece + n, 16), size)

    def zcopies(h):
        return (
            xcopy(4, h, zs.at[h, 0], za.at[h], zp),
            xcopy(5, h, zs.at[h, 1], zb.at[h], zm),
            xcopy(6, h, zt.at[h, 0], zl_.at[h], zp),
            xcopy(7, h, zt.at[h, 1], zr_.at[h], zm),
        )

    for h in range(2):
        for one in bcopy(h):
            one.wait_recv()
        tz[h] = (own[h] + xl[h].astype(F32) + xr[h].astype(F32)).T
        zs[h, 0] = tz[h, zrows(2, 0, low)].astype(BF16)
        zs[h, 1] = tz[h, zrows(2, low, low)].astype(BF16)
        for one in zcopies(h)[:2]:
            one.start()
    for h in range(2):
        first, second, third, fourth = zcopies(h)
        first.wait_recv()
        zt[h, 0, :low] = (tz[h, zrows(1, 0, low)] + za[h].astype(F32)).astype(BF16)
        zt[h, 0, low:] = tz[h, zrows(1, low, low)].astype(BF16)
        third.start()
        second.wait_recv()
        zt[h, 1, :low] = tz[h, zrows(3, 0, low)].astype(BF16)
        zt[h, 1, low:] = (tz[h, zrows(3, low, low)] + zb[h].astype(F32)).astype(BF16)
        fourth.start()
    for h in range(2):
        for one in zcopies(h)[2:]:
            one.wait_recv()
        out[:, h * hrows : (h + 1) * hrows] = (
            tz[h, zrows(0, 0, piece)] + zl_[h].astype(F32) + zr_[h].astype(F32)
        )

    for make, cond in sent:
        if cond is None:
            make().wait_send()
        else:
            pl.when(cond)(lambda: make().wait_send())
    for h in range(2):
        for one in acopy(h) + bcopy(h) + zcopies(h):
            one.wait_send()


def on_device(bra, ket, coll, kern, weight, group, occupied):
    bra_t, ket_t = bra[0].T, ket[0].T
    occ, mm = bra_t.shape
    rows = coll.shape[0]
    hrows, qrows, width = rows // 2, rows // 4, mm // 4
    piece = width // 4
    vmem = pl.BlockSpec(memory_space=pltpu.VMEM)
    smem = pl.BlockSpec(memory_space=pltpu.SMEM)
    dma = pltpu.SemaphoreType.DMA
    result = pl.pallas_call(
        kernel,
        out_shape=jax.ShapeDtypeStruct((piece, rows), F32),
        in_specs=[smem, smem, smem, vmem, vmem, vmem, pl.BlockSpec(memory_space=pl.ANY)],
        out_specs=vmem,
        scratch_shapes=[
            pltpu.VMEM((4, 2, occ, mm), BF16),
            pltpu.VMEM((4, 4, 2, occ, rows), BF16),
            pltpu.VMEM((4, 2, rows, occ), BF16),
            pltpu.VMEM((4, rows, rows), BF16),
            pltpu.VMEM((4, 2, rows, occ), F32),
            pltpu.VMEM((4, 8, 256), F32),
            pltpu.VMEM((4, 8, 256), F32),
            pltpu.VMEM((hrows, width), F32),
            pltpu.VMEM((2, 3, hrows, width), BF16),
            pltpu.VMEM((2, qrows, width), BF16),
            pltpu.VMEM((2, qrows, width), BF16),
            pltpu.VMEM((2, hrows, width), BF16),
            pltpu.VMEM((2, hrows, width), BF16),
            pltpu.VMEM((2, hrows, width), F32),
            pltpu.VMEM((2, width, hrows), F32),
            pltpu.VMEM((2, 2, piece // 2, hrows), BF16),
            pltpu.VMEM((2, 2, piece, hrows), BF16),
            pltpu.VMEM((2, piece // 2, hrows), BF16),
            pltpu.VMEM((2, piece // 2, hrows), BF16),
            pltpu.VMEM((2, piece, hrows), BF16),
            pltpu.VMEM((2, piece, hrows), BF16),
            dma((12,)), dma((12,)), dma((9, 4)), dma((9, 4)), dma((6,)), dma((6,)),
            dma((6,)), dma((6,)), dma((8, 2)), dma((8, 2)), dma,
        ],
        compiler_params=pltpu.CompilerParams(
            collective_id=0, has_side_effects=True, vmem_limit_bytes=67043328
        ),
    )(weight, group, occupied, bra_t, ket_t, coll, kern)
    return result.T


def solution(mesh):
    in_specs = (
        P("walk", None, None),
        P("walk", None, None),
        P("pt", None),
        P("pt", "walk"),
        P("walk"),
        P("walk"),
        P(),
    )
    return jax.shard_map(
        on_device, mesh=mesh, in_specs=in_specs, out_specs=P("pt", "walk"), check_vma=False
    )
```

```python
import jax
import jax.numpy as jnp
from jax import lax
from jax.experimental import pallas as pl
from jax.experimental.pallas import tpu as pltpu
from jax.sharding import PartitionSpec as P

MESH = pl.DeviceIdType.MESH
F32 = jnp.float32
BF16 = jnp.bfloat16
NT = (((1,), (1,)), ((), ()))
TILE = 256
ORDER = (
    ("o", 0), ("yh", 0), ("s1a",), ("rh", 0), ("s1b",), ("yo", 0), ("s2a",), ("o", 1), ("ro", 0), ("P", 1),
    ("s2b",), ("w",), ("U", 0, 0), ("s3",), ("yo", 1), ("yh", 1), ("kr",), ("o", 2), ("P", 2), ("U", 0, 2),
    ("rh", 1), ("ro", 1), ("s4",), ("U", 0, 1), ("U", 1, 1), ("yo", 2), ("yh", 2), ("P", 3), ("o", 3),
    ("U", 1, 0), ("ro", 2), ("U", 1, 2), ("rh", 2), ("U", 1, 3), ("yh", 3), ("U", 2, 0), ("yo", 3),
    ("U", 2, 3), ("rh", 3), ("U", 2, 1), ("U", 2, 2), ("ro", 3), ("U", 0, 3),
)


def kernel(
    weight, group, occupied, bra, ket, coll, kern, out,
    vt, lta, lb, kb, grad, lend, wz, wx, chunk, po, xa, xb, xl, xr, own, tz, zs, zt, za, zb, zl_, zr_,
    vs, vr, ls, lr, ks_, kr, ws, wr, os_, or_, loc,
):
    wi, pi = lax.axis_index("walk"), lax.axis_index("pt")
    x, zh, y, s = wi // 4, wi % 4, pi // 4, pi % 4
    zl, c = s // 2, s % 2
    occ, mm, rows = bra.shape[0], bra.shape[1], coll.shape[0]
    half = occ // 2
    krows = rows // 2

    def dev(x_, zh_, y_, s_):
        return {"walk": x_ * 4 + zh_, "pt": y_ * 4 + s_}

    xp, xm, x2 = (dev((x + d) % 4, zh, y, s) for d in (1, 3, 2))
    zp, zm, z2 = (dev(x, (zh + d) % 4, y, s) for d in (1, 3, 2))
    yp, ym = (dev(x, zh, (y + d) % 4, s) for d in (1, 3))
    oz = (zh * 2 + zl + 7 + 2 * zl) % 8
    outer = dev(x, oz // 2, y, (oz % 2) * 2 + c)
    inner = dev(x, zh, y, (1 - zl) * 2 + c)
    mate = dev(x, zh, y, zl * 2 + 1 - c)
    ro, ri = 3 - 2 * zl, 1 + 2 * zl
    slots = (0, ro, ri, 2)
    hf = pl.ds(pl.multiple_of(half * (1 - zl), 16), half)
    ho = pl.ds(pl.multiple_of(half * zl, 16), half)
    home = s == zh
    lead = c == zh % 2
    other = jnp.logical_and(lead, s != zh)
    helper = (zh - s + 4) % 4 == ri

    barrier = pltpu.get_barrier_semaphore()
    peers = (xp, xm, x2, zp, zm, z2, yp, ym, outer, inner, mate)
    for peer in peers:
        pl.semaphore_signal(barrier, inc=1, device_id=peer, device_id_type=MESH)

    sent = []

    def copy(src, dst, send, recv, to):
        return pltpu.make_async_remote_copy(
            src_ref=src, dst_ref=dst, send_sem=send, recv_sem=recv, device_id=to,
            device_id_type=MESH,
        )

    def send(make, cond=None):
        make().start()
        sent.append((make, cond))

    live = lax.broadcasted_iota(jnp.int32, (occ, mm), 0) < occupied[group[0]]
    vt[0, 0] = jnp.where(live, bra[...], jnp.zeros_like(bra[...]))
    vt[0, 1] = jnp.where(live, ket[...], jnp.zeros_like(ket[...]))
    wz[0] = jnp.full(wz.shape[1:], weight[0], F32)
    local = pltpu.make_async_copy(kern, kb.at[0], loc)
    local.start()

    def kpart(i, slot, n):
        return kb.at[slot, pl.ds(n * krows, krows)]

    def kcopy(i, slot, n, to, src=None):
        src = kern.at[pl.ds(n * krows, krows)] if src is None else src
        return copy(src, kpart(i, slot, n), ks_.at[i], kr.at[i], to)

    def vcopy(i, src_slot, slot, side, part, to):
        return copy(
            vt.at[src_slot, side, part], vt.at[slot, side, part], vs.at[i], vr.at[i], to
        )

    def vwait(i, slot, side, part, to):
        vcopy(i, slot, slot, side, part, to).wait_recv()

    def s1a():
        vwait(0, ro, c, ho, outer)
        send(lambda: vcopy(2, ro, ro, c, ho, inner))
        send(lambda: vcopy(6, ro, ro, c, ho, mate))

    def s1b():
        vwait(1, ro, c, hf, outer)
        send(lambda: vcopy(3, ro, ro, c, hf, inner))
        send(lambda: vcopy(7, ro, ro, c, hf, mate))

    def s2a():
        vwait(2, ri, c, hf, inner)
        send(lambda: vcopy(4, ri, 2, c, hf, outer))
        send(lambda: vcopy(8, ri, ri, c, hf, mate))

    def s2b():
        vwait(3, ri, c, ho, inner)
        send(lambda: vcopy(9, ri, ri, c, ho, mate))

    def s3():
        vwait(4, 2, c, ho, outer)
        send(lambda: vcopy(5, 2, 2, c, ho, inner))
        send(lambda: vcopy(10, 2, 2, c, ho, mate))

    def s4():
        vwait(5, 2, c, hf, inner)
        send(lambda: vcopy(11, 2, 2, c, hf, mate))

    def vmate(kk):
        slot = slots[kk]
        first, second = ((ho, hf), (hf, ho), (ho, hf))[kk - 1]
        vwait(4 + 2 * kk, slot, 1 - c, first, mate)
        vwait(5 + 2 * kk, slot, 1 - c, second, mate)

    def krelay():
        kcopy(0, 3, 0, xp).wait_recv()
        send(lambda: kcopy(4, 2, 0, xp, kpart(0, 3, 0)))
        kcopy(1, 1, 1, xm).wait_recv()
        send(lambda: kcopy(5, 2, 1, xm, kpart(1, 1, 1)))

    def lcopy(i, src, dst, slot, to):
        return copy(src, dst, ls.at[i, slot], lr.at[i, slot], to)

    def spread(kk, cond):
        slot = slots[kk]
        send(lambda: lcopy(1, lta.at[0, slot], lta.at[3, slot], slot, yp), cond)
        send(lambda: lcopy(2, lta.at[0, slot], lta.at[1, slot], slot, ym), cond)
        send(lambda: lcopy(5, lta.at[0, slot], lta.at[0, slot], slot, mate), cond)

    def give(kk):
        slot = slots[kk]

        @pl.when(home)
        def _():
            if kk < 2:
                send(lambda: lcopy(0, lta.at[0, slot], lta.at[0, slot], slot, inner), home)
            spread(kk, home)

        if kk in (0, 2):

            @pl.when(helper)
            def _():
                to = ri if kk == 0 else 2
                send(lambda: copy(
                    lend.at[kk // 2], lta.at[0, to], ls.at[9, kk], lr.at[0, to], outer
                ), helper)

    def take(kk):
        @pl.when(other)
        def _():
            slot = slots[kk]
            here = lta.at[0, slot]
            lcopy(0, here, here, slot, inner).wait_recv()
            spread(kk, other)

    def yrelay(kk, cond):
        @pl.when(cond)
        def _():
            slot = slots[kk]
            low, high = lta.at[3, slot], lta.at[1, slot]
            lcopy(1, low, low, slot, yp).wait_recv()
            send(lambda: lcopy(3, lta.at[3, slot, 0], lta.at[2, slot, 0], slot, yp), cond)
            send(lambda: lcopy(8, lta.at[3, slot], lta.at[3, slot], slot, mate), cond)
            lcopy(2, high, high, slot, ym).wait_recv()
            send(lambda: lcopy(4, lta.at[1, slot, 1], lta.at[2, slot, 1], slot, ym), cond)
            send(lambda: lcopy(6, lta.at[1, slot], lta.at[1, slot], slot, mate), cond)

    def far(kk, cond):
        @pl.when(cond)
        def _():
            slot = slots[kk]
            one, two = lta.at[2, slot, 0], lta.at[2, slot, 1]
            lcopy(3, one, one, slot, yp).wait_recv()
            lcopy(4, two, two, slot, ym).wait_recv()
            send(lambda: lcopy(7, lta.at[2, slot], lta.at[2, slot], slot, mate), cond)

    def weights():
        for d, to in ((1, zp), (2, z2), (3, zm)):
            copy(wz.at[4 - d], wz.at[4 - d], ws.at[d - 1], wr.at[d - 1], to).wait_recv()
        wx[0] = wz[0] + wz[1] + wz[2] + wz[3]
        for d, to in ((1, xp), (2, x2), (3, xm)):
            send(lambda d=d, to=to: copy(wx.at[0], wx.at[4 - d], ws.at[d + 2], wr.at[d + 2], to))

    calls = {
        "s1a": s1a, "s1b": s1b, "s2a": s2a, "s2b": s2b, "s3": s3, "s4": s4, "kr": krelay, "w": weights,
        "o": take, "yh": lambda kk: yrelay(kk, home), "yo": lambda kk: yrelay(kk, other),
        "rh": lambda kk: far(kk, home), "ro": lambda kk: far(kk, other),
    }

    def tri(n):
        return (n * (n + 1) // 2) % 4

    def project(kk):
        slot = (tri(kk) * ro) % 4
        both = vt[slot].reshape(2 * occ, mm)
        pts = lax.dot_general(both, coll[...], NT, preferred_element_type=F32).astype(BF16)
        for side in range(2):
            lb[slot, side] = pts[side * occ : (side + 1) * occ].T

        @pl.when(home)
        def _():
            lta[0, slot] = pts.reshape(2, occ, rows)

        @pl.when(jnp.logical_and(helper, kk % 2 == 0))
        def _():
            lend[kk // 2] = pts.reshape(2, occ, rows)

    def arrived(kk, jj):
        @pl.when(jnp.logical_not(lead))
        def _():
            slot = (tri(kk) * ro) % 4
            yr = (x + tri(jj) - y + 4) % 4
            here = lta.at[yr, slot]
            lcopy(5 + yr, here, here, slot, mate).wait_recv()

    def unit(kk, jj, part):
        slot = (tri(kk) * ro) % 4
        j = tri(jj)
        yr = (x + j - y + 4) % 4

        total = [None, None]
        for q in range(rows // TILE):
            cols = pl.ds(q * TILE, TILE)
            kq = kb[j, part, cols].astype(F32)
            for side in range(2):
                green = jnp.dot(
                    lb[slot, side, part], lta[yr, slot, 1 - side, :, cols], preferred_element_type=F32
                )
                had = (kq * green).astype(BF16)
                more = lax.dot_general(
                    had, lta[yr, slot, side, :, cols], NT, preferred_element_type=F32
                )
                total[side] = more if total[side] is None else total[side] + more
        for side in range(2):
            grad[slot, side, part] += total[1 - side]

    for slot in range(4):
        for side in range(2):
            grad[slot, side] = jnp.zeros(grad.shape[2:], F32)

    project(0)
    pl.semaphore_wait(barrier, len(peers))
    send(lambda: vcopy(0, 0, ri, c, hf, outer))
    send(lambda: kcopy(0, 3, 0, xp))
    send(lambda: kcopy(1, 1, 1, xm))
    send(lambda: vcopy(1, 0, ri, c, ho, outer))
    send(lambda: kcopy(2, 3, 1, xp))
    send(lambda: kcopy(3, 1, 0, xm))
    for d, to in ((1, zp), (2, z2), (3, zm)):
        send(lambda d=d, to=to: copy(wz.at[0], wz.at[4 - d], ws.at[d - 1], wr.at[d - 1], to))
    give(0)

    steps, ahead, first = [], [], set()
    for token in ORDER:
        if token[0] not in ("P", "U"):
            ahead.append(token)
            continue
        ids = ()
        if token[0] == "U" and token[2] not in first:
            first.add(token[2])
            ids = ((), ((3, 1, 0, xm),), ((2, 3, 1, xp),), ((4, 2, 0, xp), (5, 2, 1, xm)))[token[2]]
        steps.append((token, ahead, ids))
        ahead = []

    def step(t, carry):
        kk, jj, proj = t * 0, t * 0, t < 0
        for n, (token, todo, ids) in enumerate(steps):
            here = t == n
            kk = jnp.where(here, token[1], kk)
            if token[0] == "P":
                proj = jnp.logical_or(proj, here)
            else:
                jj = jnp.where(here, token[2], jj)
            if not todo and not ids and n:
                continue

            @pl.when(here)
            def _():
                for one in todo:
                    calls[one[0]](*one[1:])
                if token[0] == "P":
                    vmate(token[1])
                for one in ids:
                    kcopy(*one).wait_recv()

        @pl.when(proj)
        def _():
            project(kk)

        for n, (token, todo, ids) in enumerate(steps):
            if token[0] == "P":

                @pl.when(t == n)
                def _():
                    give(token[1])

        @pl.when(jnp.logical_not(proj))
        def _():
            arrived(kk, jj)
            unit(kk, jj, pl.ds(0, rows))

        return carry

    local.wait()
    lax.fori_loop(0, len(steps), step, 0)

    for d, to in ((1, xp), (2, x2), (3, xm)):
        copy(wx.at[4 - d], wx.at[4 - d], ws.at[d + 2], wr.at[d + 2], to).wait_recv()
    whole = wx[0] + wx[1] + wx[2] + wx[3]

    hrows = rows // 2
    qrows = rows // 4
    width = mm // 4
    piece = width // 4

    def xcopy(i, h, src, dst, to):
        return copy(src, dst, os_.at[i, h], or_.at[i, h], to)

    def acopy(h):
        return (
            xcopy(0, h, po.at[h, 0, pl.ds(0, qrows)], xa.at[h], xp),
            xcopy(1, h, po.at[h, 0, pl.ds(qrows, qrows)], xb.at[h], xm),
        )

    def bcopy(h):
        return xcopy(2, h, po.at[h, 1], xl.at[h], xp), xcopy(3, h, po.at[h, 2], xr.at[h], xm)

    def part_of(h):
        return pl.ds(pl.multiple_of(h * hrows, 16), hrows)

    def last(h, jjs):
        def one(jj, carry):
            unit(3, jj, part_of(h))
            return carry

        lax.fori_loop(jjs[0], jjs[1], one, 0)

    def scale(h):
        def one(i, carry):
            slot, side = i // 2, i % 2
            share = (2.0 * wz[slot] / whole)[0:1, :occ]
            lb[slot, side, part_of(h)] = (grad[slot, side, part_of(h)] * share).astype(BF16)
            return carry

        lax.fori_loop(0, 8, one, 0)

    def term(h, d):
        cols = pl.ds(pl.multiple_of(((x + d) % 4) * width, 128), width)
        acc = None
        for slot in range(4):
            for side in range(2):
                one = jnp.dot(
                    lb[slot, side, part_of(h)], vt[slot, side, :, cols], preferred_element_type=F32
                )
                acc = one if acc is None else acc + one
        return acc

    def send_far(h):
        po[h, 0] = term(h, 2).astype(BF16)
        for one in acopy(h):
            one.start()

    def send_up(h):
        chunk[...] = term(h, 1)
        acopy(h)[0].wait_recv()
        po[h, 1, :qrows] = (chunk[:qrows] + xa[h].astype(F32)).astype(BF16)
        po[h, 1, qrows:] = chunk[qrows:].astype(BF16)
        bcopy(h)[0].start()

    def send_down(h):
        chunk[...] = term(h, 3)
        acopy(h)[1].wait_recv()
        po[h, 2, :qrows] = chunk[:qrows].astype(BF16)
        po[h, 2, qrows:] = (chunk[qrows:] + xb[h].astype(F32)).astype(BF16)
        bcopy(h)[1].start()

    def keep_own(h):
        own[h] = term(h, 0)

    low = piece // 2

    def zrows(d, n, size):
        return pl.ds(pl.multiple_of(((zh + d) % 4) * piece + n, 16), size)

    def zcopies(h):
        return (
            xcopy(4, h, zs.at[h, 0], za.at[h], zp),
            xcopy(5, h, zs.at[h, 1], zb.at[h], zm),
            xcopy(6, h, zt.at[h, 0], zl_.at[h], zp),
            xcopy(7, h, zt.at[h, 1], zr_.at[h], zm),
        )

    def gather(h):
        for one in bcopy(h):
            one.wait_recv()
        tz[h] = (own[h] + xl[h].astype(F32) + xr[h].astype(F32)).T
        zs[h, 0] = tz[h, zrows(2, 0, low)].astype(BF16)
        zs[h, 1] = tz[h, zrows(2, low, low)].astype(BF16)
        for one in zcopies(h)[:2]:
            one.start()

    def turn(h):
        first, second, third, fourth = zcopies(h)
        first.wait_recv()
        zt[h, 0, :low] = (tz[h, zrows(1, 0, low)] + za[h].astype(F32)).astype(BF16)
        zt[h, 0, low:] = tz[h, zrows(1, low, low)].astype(BF16)
        third.start()
        second.wait_recv()
        zt[h, 1, :low] = tz[h, zrows(3, 0, low)].astype(BF16)
        zt[h, 1, low:] = (tz[h, zrows(3, low, low)] + zb[h].astype(F32)).astype(BF16)
        fourth.start()

    def finish(h):
        for one in zcopies(h)[2:]:
            one.wait_recv()
        out[:, h * hrows : (h + 1) * hrows] = (
            tz[h, zrows(0, 0, piece)] + zl_[h].astype(F32) + zr_[h].astype(F32)
        )

    for jj in range(4):
        arrived(3, jj)
    last(0, (0, 4))
    scale(0)
    send_far(0)
    last(1, (0, 2))
    send_up(0)
    send_down(0)
    last(1, (2, 4))
    scale(1)
    send_far(1)
    keep_own(0)
    gather(0)
    send_up(1)
    turn(0)
    send_down(1)
    keep_own(1)
    finish(0)
    gather(1)
    turn(1)
    finish(1)

    for make, cond in sent:
        if cond is None:
            make().wait_send()
        else:
            pl.when(cond)(lambda: make().wait_send())
    for h in range(2):
        for one in acopy(h) + bcopy(h) + zcopies(h):
            one.wait_send()


def on_device(bra, ket, coll, kern, weight, group, occupied):
    bra_t, ket_t = bra[0].T, ket[0].T
    occ, mm = bra_t.shape
    rows = coll.shape[0]
    hrows, qrows, width = rows // 2, rows // 4, mm // 4
    piece = width // 4
    vmem = pl.BlockSpec(memory_space=pltpu.VMEM)
    smem = pl.BlockSpec(memory_space=pltpu.SMEM)
    dma = pltpu.SemaphoreType.DMA
    result = pl.pallas_call(
        kernel,
        out_shape=jax.ShapeDtypeStruct((piece, rows), F32),
        in_specs=[smem, smem, smem, vmem, vmem, vmem, pl.BlockSpec(memory_space=pl.ANY)],
        out_specs=vmem,
        scratch_shapes=[
            pltpu.VMEM((4, 2, occ, mm), BF16),
            pltpu.VMEM((4, 4, 2, occ, rows), BF16),
            pltpu.VMEM((4, 2, rows, occ), BF16),
            pltpu.VMEM((4, rows, rows), BF16),
            pltpu.VMEM((4, 2, rows, occ), F32),
            pltpu.VMEM((2, 2, occ, rows), BF16),
            pltpu.VMEM((4, 8, 256), F32),
            pltpu.VMEM((4, 8, 256), F32),
            pltpu.VMEM((hrows, width), F32),
            pltpu.VMEM((2, 3, hrows, width), BF16),
            pltpu.VMEM((2, qrows, width), BF16),
            pltpu.VMEM((2, qrows, width), BF16),
            pltpu.VMEM((2, hrows, width), BF16),
            pltpu.VMEM((2, hrows, width), BF16),
            pltpu.VMEM((2, hrows, width), F32),
            pltpu.VMEM((2, width, hrows), F32),
            pltpu.VMEM((2, 2, piece // 2, hrows), BF16),
            pltpu.VMEM((2, 2, piece, hrows), BF16),
            pltpu.VMEM((2, piece // 2, hrows), BF16),
            pltpu.VMEM((2, piece // 2, hrows), BF16),
            pltpu.VMEM((2, piece, hrows), BF16),
            pltpu.VMEM((2, piece, hrows), BF16),
            dma((12,)), dma((12,)), dma((10, 4)), dma((9, 4)), dma((6,)), dma((6,)),
            dma((6,)), dma((6,)), dma((8, 2)), dma((8, 2)), dma,
        ],
        compiler_params=pltpu.CompilerParams(
            collective_id=0, has_side_effects=True, vmem_limit_bytes=67043328
        ),
    )(weight, group, occupied, bra_t, ket_t, coll, kern)
    return result.T


def solution(mesh):
    in_specs = (
        P("walk", None, None),
        P("walk", None, None),
        P("pt", None),
        P("pt", "walk"),
        P("walk"),
        P("walk"),
        P(),
    )
    return jax.shard_map(
        on_device, mesh=mesh, in_specs=in_specs, out_specs=P("pt", "walk"), check_vma=False
    )
```

```python
import jax
import jax.numpy as jnp
from jax import lax
from jax.experimental import pallas as pl
from jax.experimental.pallas import tpu as pltpu
from jax.sharding import PartitionSpec as P

MESH = pl.DeviceIdType.MESH
F32 = jnp.float32
BF16 = jnp.bfloat16
NT = (((1,), (1,)), ((), ()))
TILE = 256
ORDER = (
    ("v0",), ("g0",), ("k0",), ("o", 0), ("yh", 0), ("s1a",), ("rh", 0), ("s1b",), ("yo", 0), ("s2a",),
    ("o", 1), ("ro", 0), ("P", 1), ("s2b",), ("w", 0), ("U", 0, 0), ("s3",), ("yo", 1), ("yh", 1), ("kr",),
    ("o", 2), ("P", 2), ("U", 0, 2), ("w", 1), ("rh", 1), ("ro", 1), ("s4",), ("U", 0, 1), ("U", 1, 1),
    ("yo", 2), ("yh", 2), ("P", 3), ("w", 2), ("o", 3), ("U", 1, 0), ("ro", 2), ("U", 1, 2), ("rh", 2),
    ("yh", 3), ("U", 2, 0), ("yo", 3), ("rh", 3), ("U", 2, 1), ("U", 2, 2), ("ro", 3), ("H", 0, 3, 0),
    ("H", 1, 3, 0), ("H", 2, 3, 0), ("H", 3, 0, 0), ("H", 3, 1, 0), ("H", 3, 2, 0), ("H", 3, 3, 0),
    ("SF", 0), ("H", 0, 3, 1), ("H", 1, 3, 1), ("H", 2, 3, 1), ("SU", 0), ("SD", 0), ("H", 3, 0, 1),
    ("H", 3, 1, 1), ("H", 3, 2, 1), ("H", 3, 3, 1), ("SF", 1), ("KO", 0), ("G", 0), ("SU", 1), ("SD", 1),
    ("T", 0), ("KO", 1), ("F", 0), ("G", 1), ("T", 1), ("F", 1),
)


def kernel(
    weight, group, occupied, bra, ket, coll, kern, out,
    vt, lta, lb, kb, grad, lend, wz, wx, chunk, po, xa, xb, xl, xr, own, tz, zs, zt, za, zb, zl_, zr_,
    vs, vr, ls, lr, ks_, kr, ws, wr, os_, or_, loc,
):
    wi, pi = lax.axis_index("walk"), lax.axis_index("pt")
    x, zh, y, s = wi // 4, wi % 4, pi // 4, pi % 4
    zl, c = s // 2, s % 2
    occ, mm, rows = bra.shape[0], bra.shape[1], coll.shape[0]
    half = occ // 2
    krows = rows // 2

    def dev(x_, zh_, y_, s_):
        return {"walk": x_ * 4 + zh_, "pt": y_ * 4 + s_}

    xp, xm = (dev((x + d) % 4, zh, y, s) for d in (1, 3))
    zp, zm = (dev(x, (zh + d) % 4, y, s) for d in (1, 3))
    yp, ym = (dev(x, zh, (y + d) % 4, s) for d in (1, 3))
    oz = (zh * 2 + zl + 7 + 2 * zl) % 8
    outer = dev(x, oz // 2, y, (oz % 2) * 2 + c)
    inner = dev(x, zh, y, (1 - zl) * 2 + c)
    mate = dev(x, zh, y, zl * 2 + 1 - c)
    ro, ri = 3 - 2 * zl, 1 + 2 * zl
    slots = (0, ro, ri, 2)
    hf = pl.ds(pl.multiple_of(half * (1 - zl), 16), half)
    ho = pl.ds(pl.multiple_of(half * zl, 16), half)
    home = s == zh
    lead = c == zh % 2
    other = jnp.logical_and(lead, s != zh)
    helper = (zh - s + 4) % 4 == ri

    barrier = pltpu.get_barrier_semaphore()
    peers = (xp, xm, zp, zm, yp, ym, outer, inner, mate)
    for peer in peers:
        pl.semaphore_signal(barrier, inc=1, device_id=peer, device_id_type=MESH)

    sent = []

    def copy(src, dst, send, recv, to):
        return pltpu.make_async_remote_copy(
            src_ref=src, dst_ref=dst, send_sem=send, recv_sem=recv, device_id=to,
            device_id_type=MESH,
        )

    def send(make, cond=None):
        make().start()
        sent.append((make, cond))

    live = lax.broadcasted_iota(jnp.int32, (occ, mm), 0) < occupied[group[0]]
    vt[0, 0] = jnp.where(live, bra[...], jnp.zeros_like(bra[...]))
    vt[0, 1] = jnp.where(live, ket[...], jnp.zeros_like(ket[...]))
    wz[0] = jnp.full(wz.shape[1:], weight[0], F32)
    local = pltpu.make_async_copy(kern, kb.at[0], loc)
    local.start()

    def kpart(i, slot, n):
        return kb.at[slot, pl.ds(n * krows, krows)]

    def kcopy(i, slot, n, to, src=None):
        src = kern.at[pl.ds(n * krows, krows)] if src is None else src
        return copy(src, kpart(i, slot, n), ks_.at[i], kr.at[i], to)

    def vcopy(i, src_slot, slot, side, part, to):
        return copy(
            vt.at[src_slot, side, part], vt.at[slot, side, part], vs.at[i], vr.at[i], to
        )

    def vwait(i, slot, side, part, to):
        vcopy(i, slot, slot, side, part, to).wait_recv()

    def s1a():
        vwait(0, ro, c, ho, outer)
        send(lambda: vcopy(2, ro, ro, c, ho, inner))
        send(lambda: vcopy(6, ro, ro, c, ho, mate))

    def s1b():
        vwait(1, ro, c, hf, outer)
        send(lambda: vcopy(3, ro, ro, c, hf, inner))
        send(lambda: vcopy(7, ro, ro, c, hf, mate))

    def s2a():
        vwait(2, ri, c, hf, inner)
        send(lambda: vcopy(4, ri, 2, c, hf, outer))
        send(lambda: vcopy(8, ri, ri, c, hf, mate))

    def s2b():
        vwait(3, ri, c, ho, inner)
        send(lambda: vcopy(9, ri, ri, c, ho, mate))

    def s3():
        vwait(4, 2, c, ho, outer)
        send(lambda: vcopy(5, 2, 2, c, ho, inner))
        send(lambda: vcopy(10, 2, 2, c, ho, mate))

    def s4():
        vwait(5, 2, c, hf, inner)
        send(lambda: vcopy(11, 2, 2, c, hf, mate))

    def vmate(kk):
        slot = slots[kk]
        first, second = ((ho, hf), (hf, ho), (ho, hf))[kk - 1]
        vwait(4 + 2 * kk, slot, 1 - c, first, mate)
        vwait(5 + 2 * kk, slot, 1 - c, second, mate)

    def krelay():
        kcopy(0, 3, 0, xp).wait_recv()
        send(lambda: kcopy(4, 2, 0, xp, kpart(0, 3, 0)))
        kcopy(1, 1, 1, xm).wait_recv()
        send(lambda: kcopy(5, 2, 1, xm, kpart(1, 1, 1)))

    def lcopy(i, src, dst, slot, to):
        return copy(src, dst, ls.at[i, slot], lr.at[i, slot], to)

    def spread(kk, cond):
        slot = slots[kk]
        send(lambda: lcopy(1, lta.at[0, slot, 0], lta.at[3, slot, 0], slot, yp), cond)
        send(lambda: lcopy(2, lta.at[0, slot, 1], lta.at[1, slot, 1], slot, ym), cond)
        send(lambda: lcopy(10, lta.at[0, slot, 1], lta.at[3, slot, 1], slot, yp), cond)
        send(lambda: lcopy(11, lta.at[0, slot, 0], lta.at[1, slot, 0], slot, ym), cond)
        send(lambda: lcopy(5, lta.at[0, slot], lta.at[0, slot], slot, mate), cond)

    def pass_on(slot, cond):
        send(lambda: lcopy(0, lta.at[0, slot], lta.at[0, slot], slot, inner), cond)

    def lend_to(i, n, slot, to, cond):
        send(lambda: copy(lend.at[n], lta.at[0, slot], ls.at[9, i], lr.at[0, slot], to), cond)

    def give(kk):
        if kk < 2:

            @pl.when(home)
            def _():
                pass_on(slots[kk], home)

        if kk in (0, 2):

            @pl.when(helper)
            def _():
                lend_to(kk, kk // 2, (ri, 2)[kk // 2], outer, helper)

        @pl.when(home)
        def _():
            spread(kk, home)

    def take(kk, cond):
        @pl.when(cond)
        def _():
            slot = slots[kk]
            here = lta.at[0, slot]
            lcopy(0, here, here, slot, inner).wait_recv()
            spread(kk, cond)

    def yrelay(kk, cond):
        @pl.when(cond)
        def _():
            slot = slots[kk]
            low, high = lta.at[3, slot], lta.at[1, slot]
            lcopy(1, low.at[0], low.at[0], slot, yp).wait_recv()
            send(lambda: lcopy(3, lta.at[3, slot, 0], lta.at[2, slot, 0], slot, yp), cond)
            lcopy(2, high.at[1], high.at[1], slot, ym).wait_recv()
            send(lambda: lcopy(4, lta.at[1, slot, 1], lta.at[2, slot, 1], slot, ym), cond)
            lcopy(10, low.at[1], low.at[1], slot, yp).wait_recv()
            send(lambda: lcopy(8, lta.at[3, slot], lta.at[3, slot], slot, mate), cond)
            lcopy(11, high.at[0], high.at[0], slot, ym).wait_recv()
            send(lambda: lcopy(6, lta.at[1, slot], lta.at[1, slot], slot, mate), cond)

    def far(kk, cond):
        @pl.when(cond)
        def _():
            slot = slots[kk]
            one, two = lta.at[2, slot, 0], lta.at[2, slot, 1]
            lcopy(3, one, one, slot, yp).wait_recv()
            lcopy(4, two, two, slot, ym).wait_recv()
            send(lambda: lcopy(7, lta.at[2, slot], lta.at[2, slot], slot, mate), cond)

    def weights(n):
        if n == 0:
            wcopy(wz, 0, 0, 3, zp).wait_recv()
            wcopy(wz, 1, 0, 1, zm).wait_recv()
            send(lambda: wcopy(wz, 2, 3, 2, zp))
        elif n == 1:
            wcopy(wz, 2, 3, 2, zp).wait_recv()
            wx[0] = wz[0] + wz[1] + wz[2] + wz[3]
            send(lambda: wcopy(wx, 3, 0, 3, xp))
            send(lambda: wcopy(wx, 4, 0, 1, xm))
        elif n == 2:
            wcopy(wx, 3, 0, 3, xp).wait_recv()
            wcopy(wx, 4, 0, 1, xm).wait_recv()
            send(lambda: wcopy(wx, 5, 3, 2, xp))
        else:
            wcopy(wx, 5, 3, 2, xp).wait_recv()

    calls = {
        "s1a": s1a, "s1b": s1b, "s2a": s2a, "s2b": s2b, "s3": s3, "s4": s4, "kr": krelay, "w": weights,
        "o": lambda kk: take(kk, other), "yh": lambda kk: yrelay(kk, home), "yo": lambda kk: yrelay(kk, other),
        "rh": lambda kk: far(kk, home), "ro": lambda kk: far(kk, other),
    }

    def tri(n):
        return (n * (n + 1) // 2) % 4

    def project(kk):
        slot = (tri(kk) * ro) % 4
        both = vt[slot].reshape(2 * occ, mm)
        pts = lax.dot_general(both, coll[...], NT, preferred_element_type=F32).astype(BF16)
        for side in range(2):
            lb[slot, side] = pts[side * occ : (side + 1) * occ].T

        @pl.when(home)
        def _():
            lta[0, slot] = pts.reshape(2, occ, rows)

        @pl.when(jnp.logical_and(helper, kk % 2 == 0))
        def _():
            lend[kk // 2] = pts.reshape(2, occ, rows)

    def arrived(kk, jj):
        @pl.when(jnp.logical_not(lead))
        def _():
            slot = (tri(kk) * ro) % 4
            yr = (x + tri(jj) - y + 4) % 4
            here = lta.at[yr, slot]
            lcopy(5 + yr, here, here, slot, mate).wait_recv()

    def unit(kk, jj, part):
        slot = (tri(kk) * ro) % 4
        j = tri(jj)
        yr = (x + j - y + 4) % 4

        total = [None, None]
        for q in range(rows // TILE):
            cols = pl.ds(q * TILE, TILE)
            kq = kb[j, part, cols].astype(F32)
            for side in range(2):
                green = jnp.dot(
                    lb[slot, side, part], lta[yr, slot, 1 - side, :, cols], preferred_element_type=F32
                )
                had = (kq * green).astype(BF16)
                more = lax.dot_general(
                    had, lta[yr, slot, side, :, cols], NT, preferred_element_type=F32
                )
                total[side] = more if total[side] is None else total[side] + more
        for side in range(2):
            grad[slot, side, part] += total[1 - side]

    for slot in range(4):
        for side in range(2):
            grad[slot, side] = jnp.zeros(grad.shape[2:], F32)

    project(0)
    pl.semaphore_wait(barrier, len(peers))
    def wcopy(buf, i, src, dst, to):
        return copy(buf.at[src], buf.at[dst], ws.at[i], wr.at[i], to)

    send(lambda: wcopy(wz, 0, 0, 3, zp))
    send(lambda: wcopy(wz, 1, 0, 1, zm))

    def orbitals():
        send(lambda: vcopy(0, 0, ri, c, hf, outer))
        send(lambda: vcopy(1, 0, ri, c, ho, outer))

    def kernels():
        send(lambda: kcopy(0, 3, 0, xp))
        send(lambda: kcopy(1, 1, 1, xm))
        send(lambda: kcopy(2, 3, 1, xp))
        send(lambda: kcopy(3, 1, 0, xm))

    calls["v0"], calls["k0"], calls["g0"] = orbitals, kernels, lambda: give(0)
    first = set()

    def run(tokens, ahead, part, waits):
        steps = []
        for token in tokens:
            if token[0] not in ("P", "U", "H"):
                ahead = ahead + [token]
                continue
            ids = ()
            if token[0] != "P" and token[2] not in first:
                first.add(token[2])
                ids = ((), ((3, 1, 0, xm),), ((2, 3, 1, xp),), ((4, 2, 0, xp), (5, 2, 1, xm)))[token[2]]
            steps.append((token, ahead, ids))
            ahead = []
        mixed = any(token[0] == "P" for token, _, _ in steps)

        def step(t, carry):
            kk, jj, proj = t * 0, t * 0, t < 0
            for n, (token, todo, ids) in enumerate(steps):
                here = t == n
                kk = jnp.where(here, token[1], kk)
                if token[0] == "P":
                    proj = jnp.logical_or(proj, here)
                else:
                    jj = jnp.where(here, token[2], jj)
                if not todo and not ids and token[0] != "P":
                    continue

                @pl.when(here)
                def _():
                    for one in todo:
                        calls[one[0]](*one[1:])
                    if token[0] == "P":
                        vmate(token[1])
                    for one in ids:
                        kcopy(*one).wait_recv()

            def block():
                if waits:
                    arrived(kk, jj)
                unit(kk, jj, part)

            if not mixed:
                block()
                return carry

            @pl.when(proj)
            def _():
                project(kk)

            for n, (token, _, _) in enumerate(steps):
                if token[0] == "P":

                    @pl.when(t == n)
                    def _():
                        give(token[1])

            pl.when(jnp.logical_not(proj))(block)
            return carry

        lax.fori_loop(0, len(steps), step, 0)
        return ahead

    order = list(ORDER)
    lasts = [n for n, token in enumerate(order) if token[0] in ("P", "U")]
    cut = lasts[-1] + 1
    cuts = [n for n, token in enumerate(order) if token[0] == "H" and token[3] == 0]
    cut2 = cuts[-1] + 1
    cuts = [n for n, token in enumerate(order) if token[0] == "H"]
    cut3 = cuts[-1] + 1
    local.wait()
    rest = run(order[:cut], [], pl.ds(0, rows), True)

    weights(3)
    whole = wx[0] + wx[1] + wx[2] + wx[3]

    hrows = rows // 2
    qrows = rows // 4
    width = mm // 4
    piece = width // 4

    def xcopy(i, h, src, dst, to):
        return copy(src, dst, os_.at[i, h], or_.at[i, h], to)

    def acopy(h):
        return (
            xcopy(0, h, po.at[h, 0, pl.ds(0, qrows)], xa.at[h], xp),
            xcopy(1, h, po.at[h, 0, pl.ds(qrows, qrows)], xb.at[h], xm),
        )

    def bcopy(h):
        return xcopy(2, h, po.at[h, 1], xl.at[h], xp), xcopy(3, h, po.at[h, 2], xr.at[h], xm)

    def part_of(h):
        return pl.ds(pl.multiple_of(h * hrows, 16), hrows)

    def scale(h):
        def one(i, carry):
            slot, side = i // 2, i % 2
            share = (2.0 * wz[slot] / whole)[0:1, :occ]
            lb[slot, side, part_of(h)] = (grad[slot, side, part_of(h)] * share).astype(BF16)
            return carry

        lax.fori_loop(0, 8, one, 0)

    def term(h, d):
        cols = pl.ds(pl.multiple_of(((x + d) % 4) * width, 128), width)
        acc = None
        for slot in range(4):
            for side in range(2):
                one = jnp.dot(
                    lb[slot, side, part_of(h)], vt[slot, side, :, cols], preferred_element_type=F32
                )
                acc = one if acc is None else acc + one
        return acc

    def send_far(h):
        po[h, 0] = term(h, 2).astype(BF16)
        for one in acopy(h):
            one.start()

    def send_up(h):
        chunk[...] = term(h, 1)
        acopy(h)[0].wait_recv()
        po[h, 1, :qrows] = (chunk[:qrows] + xa[h].astype(F32)).astype(BF16)
        po[h, 1, qrows:] = chunk[qrows:].astype(BF16)
        bcopy(h)[0].start()

    def send_down(h):
        chunk[...] = term(h, 3)
        acopy(h)[1].wait_recv()
        po[h, 2, :qrows] = chunk[:qrows].astype(BF16)
        po[h, 2, qrows:] = (chunk[qrows:] + xb[h].astype(F32)).astype(BF16)
        bcopy(h)[1].start()

    def keep_own(h):
        own[h] = term(h, 0)

    low = piece // 2

    def zrows(d, n, size):
        return pl.ds(pl.multiple_of(((zh + d) % 4) * piece + n, 16), size)

    def zcopies(h):
        return (
            xcopy(4, h, zs.at[h, 0], za.at[h], zp),
            xcopy(5, h, zs.at[h, 1], zb.at[h], zm),
            xcopy(6, h, zt.at[h, 0], zl_.at[h], zp),
            xcopy(7, h, zt.at[h, 1], zr_.at[h], zm),
        )

    def gather(h):
        for one in bcopy(h):
            one.wait_recv()
        tz[h] = (own[h] + xl[h].astype(F32) + xr[h].astype(F32)).T
        zs[h, 0] = tz[h, zrows(2, 0, low)].astype(BF16)
        zs[h, 1] = tz[h, zrows(2, low, low)].astype(BF16)
        for one in zcopies(h)[:2]:
            one.start()

    def turn(h):
        first, second, third, fourth = zcopies(h)
        first.wait_recv()
        zt[h, 0, :low] = (tz[h, zrows(1, 0, low)] + za[h].astype(F32)).astype(BF16)
        zt[h, 0, low:] = tz[h, zrows(1, low, low)].astype(BF16)
        third.start()
        second.wait_recv()
        zt[h, 1, :low] = tz[h, zrows(3, 0, low)].astype(BF16)
        zt[h, 1, low:] = (tz[h, zrows(3, low, low)] + zb[h].astype(F32)).astype(BF16)
        fourth.start()

    def finish(h):
        for one in zcopies(h)[2:]:
            one.wait_recv()
        out[:, h * hrows : (h + 1) * hrows] = (
            tz[h, zrows(0, 0, piece)] + zl_[h].astype(F32) + zr_[h].astype(F32)
        )

    def far_first(h):
        scale(h)
        send_far(h)

    calls.update(SF=far_first, SU=send_up, SD=send_down, KO=keep_own, G=gather, T=turn, F=finish)
    rest = run(order[cut:cut2], rest, pl.ds(0, hrows), True)
    rest = run(order[cut2:cut3], rest, pl.ds(hrows, hrows), False)
    for one in rest + order[cut3:]:
        calls[one[0]](*one[1:])

    for make, cond in sent:
        if cond is None:
            make().wait_send()
        else:
            pl.when(cond)(lambda: make().wait_send())
    for h in range(2):
        for one in acopy(h) + bcopy(h) + zcopies(h):
            one.wait_send()


def on_device(bra, ket, coll, kern, weight, group, occupied):
    bra_t, ket_t = bra[0].T, ket[0].T
    occ, mm = bra_t.shape
    rows = coll.shape[0]
    hrows, qrows, width = rows // 2, rows // 4, mm // 4
    piece = width // 4
    vmem = pl.BlockSpec(memory_space=pltpu.VMEM)
    smem = pl.BlockSpec(memory_space=pltpu.SMEM)
    dma = pltpu.SemaphoreType.DMA
    result = pl.pallas_call(
        kernel,
        out_shape=jax.ShapeDtypeStruct((piece, rows), F32),
        in_specs=[smem, smem, smem, vmem, vmem, vmem, pl.BlockSpec(memory_space=pl.ANY)],
        out_specs=vmem,
        scratch_shapes=[
            pltpu.VMEM((4, 2, occ, mm), BF16),
            pltpu.VMEM((4, 4, 2, occ, rows), BF16),
            pltpu.VMEM((4, 2, rows, occ), BF16),
            pltpu.VMEM((4, rows, rows), BF16),
            pltpu.VMEM((4, 2, rows, occ), F32),
            pltpu.VMEM((2, 2, occ, rows), BF16),
            pltpu.VMEM((4, 8, 256), F32),
            pltpu.VMEM((4, 8, 256), F32),
            pltpu.VMEM((hrows, width), F32),
            pltpu.VMEM((2, 3, hrows, width), BF16),
            pltpu.VMEM((2, qrows, width), BF16),
            pltpu.VMEM((2, qrows, width), BF16),
            pltpu.VMEM((2, hrows, width), BF16),
            pltpu.VMEM((2, hrows, width), BF16),
            pltpu.VMEM((2, hrows, width), F32),
            pltpu.VMEM((2, width, hrows), F32),
            pltpu.VMEM((2, 2, piece // 2, hrows), BF16),
            pltpu.VMEM((2, 2, piece, hrows), BF16),
            pltpu.VMEM((2, piece // 2, hrows), BF16),
            pltpu.VMEM((2, piece // 2, hrows), BF16),
            pltpu.VMEM((2, piece, hrows), BF16),
            pltpu.VMEM((2, piece, hrows), BF16),
            dma((12,)), dma((12,)), dma((12, 4)), dma((12, 4)), dma((6,)), dma((6,)),
            dma((6,)), dma((6,)), dma((8, 2)), dma((8, 2)), dma,
        ],
        compiler_params=pltpu.CompilerParams(
            collective_id=0, has_side_effects=True, vmem_limit_bytes=67043328
        ),
    )(weight, group, occupied, bra_t, ket_t, coll, kern)
    return result.T


def solution(mesh):
    in_specs = (
        P("walk", None, None),
        P("walk", None, None),
        P("pt", None),
        P("pt", "walk"),
        P("walk"),
        P("walk"),
        P(),
    )
    return jax.shard_map(
        on_device, mesh=mesh, in_specs=in_specs, out_specs=P("pt", "walk"), check_vma=False
    )
```

```python
import jax
import jax.numpy as jnp
from jax import lax
from jax.experimental import pallas as pl
from jax.experimental.pallas import tpu as pltpu
from jax.sharding import PartitionSpec as P

MESH = pl.DeviceIdType.MESH
F32 = jnp.float32
BF16 = jnp.bfloat16
NT = (((1,), (1,)), ((), ()))
TILE = 256
ORDER = (
    ("v0",), ("g0",), ("k0",), ("o", 0), ("yh", 0), ("s1a",), ("rh", 0), ("s1b",), ("yo", 0), ("s2a",),
    ("o", 1), ("ro", 0), ("P", 1), ("s2b",), ("w", 0), ("kr",), ("U", 0, 0), ("s3",), ("yo", 1), ("yh", 1),
    ("o", 2), ("P", 2), ("w", 1), ("U", 0, 2), ("rh", 1), ("ro", 1), ("s4",), ("U", 0, 1), ("U", 1, 1),
    ("yo", 2), ("yh", 2), ("P", 3), ("w", 2), ("o", 3), ("U", 1, 0), ("ro", 2), ("U", 1, 2), ("rh", 2),
    ("yh", 3), ("U", 2, 0), ("yo", 3), ("rh", 3), ("U", 2, 1), ("U", 2, 2), ("ro", 3), ("H", 0, 3, 0),
    ("H", 1, 3, 0), ("H", 2, 3, 0), ("H", 3, 0, 0), ("H", 3, 1, 0), ("H", 3, 2, 0), ("H", 3, 3, 0),
    ("SF", 0), ("H", 0, 3, 1), ("H", 1, 3, 1), ("H", 2, 3, 1), ("H", 3, 0, 1), ("SU", 0), ("SD", 0),
    ("H", 3, 1, 1), ("H", 3, 2, 1), ("H", 3, 3, 1), ("SF", 1), ("SU", 1), ("SD", 1), ("KO", 0), ("KO", 1),
    ("G", 0), ("G", 1), ("T", 0), ("T", 1), ("F", 0), ("F", 1),
)


def kernel(
    weight, group, occupied, bra, ket, coll, kern, out,
    vt, lta, lb, kb, grad, lend, wz, wx, chunk, po, xa, xb, xl, xr, own, tz, zs, zt, za, zb, zl_, zr_,
    vs, vr, ls, lr, ks_, kr, ws, wr, os_, or_, loc,
):
    wi, pi = lax.axis_index("walk"), lax.axis_index("pt")
    x, zh, y, s = wi // 4, wi % 4, pi // 4, pi % 4
    zl, c = s // 2, s % 2
    occ, mm, rows = bra.shape[0], bra.shape[1], coll.shape[0]
    half = occ // 2
    krows = rows // 2

    def dev(x_, zh_, y_, s_):
        return {"walk": x_ * 4 + zh_, "pt": y_ * 4 + s_}

    xp, xm = (dev((x + d) % 4, zh, y, s) for d in (1, 3))
    zp, zm = (dev(x, (zh + d) % 4, y, s) for d in (1, 3))
    yp, ym = (dev(x, zh, (y + d) % 4, s) for d in (1, 3))
    oz = (zh * 2 + zl + 7 + 2 * zl) % 8
    outer = dev(x, oz // 2, y, (oz % 2) * 2 + c)
    inner = dev(x, zh, y, (1 - zl) * 2 + c)
    mate = dev(x, zh, y, zl * 2 + 1 - c)
    ro, ri = 3 - 2 * zl, 1 + 2 * zl
    slots = (0, ro, ri, 2)
    hf = pl.ds(pl.multiple_of(half * (1 - zl), 16), half)
    ho = pl.ds(pl.multiple_of(half * zl, 16), half)
    home = s == zh
    lead = c == zh % 2
    other = jnp.logical_and(lead, s != zh)
    helper = (zh - s + 4) % 4 == ri

    barrier = pltpu.get_barrier_semaphore()
    peers = (xp, xm, zp, zm, yp, ym, outer, inner, mate)
    for peer in peers:
        pl.semaphore_signal(barrier, inc=1, device_id=peer, device_id_type=MESH)

    sent = []

    def copy(src, dst, send, recv, to):
        return pltpu.make_async_remote_copy(
            src_ref=src, dst_ref=dst, send_sem=send, recv_sem=recv, device_id=to,
            device_id_type=MESH,
        )

    def send(make, cond=None):
        make().start()
        sent.append((make, cond))

    live = lax.broadcasted_iota(jnp.int32, (occ, mm), 0) < occupied[group[0]]
    vt[0, 0] = jnp.where(live, bra[...], jnp.zeros_like(bra[...]))
    vt[0, 1] = jnp.where(live, ket[...], jnp.zeros_like(ket[...]))
    wz[0] = jnp.full(wz.shape[1:], weight[0], F32)
    local = pltpu.make_async_copy(kern, kb.at[0], loc)
    local.start()

    def kpart(i, slot, n):
        return kb.at[slot, pl.ds(n * krows, krows)]

    def kcopy(i, slot, n, to, src=None):
        src = kern.at[pl.ds(n * krows, krows)] if src is None else src
        return copy(src, kpart(i, slot, n), ks_.at[i], kr.at[i], to)

    def vcopy(i, src_slot, slot, side, part, to):
        return copy(
            vt.at[src_slot, side, part], vt.at[slot, side, part], vs.at[i], vr.at[i], to
        )

    def vwait(i, slot, side, part, to):
        vcopy(i, slot, slot, side, part, to).wait_recv()

    def s1a():
        vwait(0, ro, c, ho, outer)
        send(lambda: vcopy(2, ro, ro, c, ho, inner))
        send(lambda: vcopy(6, ro, ro, c, ho, mate))

    def s1b():
        vwait(1, ro, c, hf, outer)
        send(lambda: vcopy(3, ro, ro, c, hf, inner))
        send(lambda: vcopy(7, ro, ro, c, hf, mate))

    def s2a():
        vwait(2, ri, c, hf, inner)
        send(lambda: vcopy(4, ri, 2, c, hf, outer))
        send(lambda: vcopy(8, ri, ri, c, hf, mate))

    def s2b():
        vwait(3, ri, c, ho, inner)
        send(lambda: vcopy(9, ri, ri, c, ho, mate))

    def s3():
        vwait(4, 2, c, ho, outer)
        send(lambda: vcopy(5, 2, 2, c, ho, inner))
        send(lambda: vcopy(10, 2, 2, c, ho, mate))

    def s4():
        vwait(5, 2, c, hf, inner)
        send(lambda: vcopy(11, 2, 2, c, hf, mate))

    def vmate(kk):
        slot = slots[kk]
        first, second = ((ho, hf), (hf, ho), (ho, hf))[kk - 1]
        vwait(4 + 2 * kk, slot, 1 - c, first, mate)
        vwait(5 + 2 * kk, slot, 1 - c, second, mate)

    def krelay():
        kcopy(0, 3, 0, xp).wait_recv()
        send(lambda: kcopy(4, 2, 0, xp, kpart(0, 3, 0)))
        kcopy(1, 1, 1, xm).wait_recv()
        send(lambda: kcopy(5, 2, 1, xm, kpart(1, 1, 1)))

    def lcopy(i, src, dst, slot, to):
        return copy(src, dst, ls.at[i, slot], lr.at[i, slot], to)

    def spread(kk, cond):
        slot = slots[kk]
        send(lambda: lcopy(1, lta.at[0, slot, 0], lta.at[3, slot, 0], slot, yp), cond)
        send(lambda: lcopy(2, lta.at[0, slot, 1], lta.at[1, slot, 1], slot, ym), cond)
        send(lambda: lcopy(10, lta.at[0, slot, 1], lta.at[3, slot, 1], slot, yp), cond)
        send(lambda: lcopy(11, lta.at[0, slot, 0], lta.at[1, slot, 0], slot, ym), cond)
        send(lambda: lcopy(5, lta.at[0, slot], lta.at[0, slot], slot, mate), cond)

    def pass_on(slot, cond):
        send(lambda: lcopy(0, lta.at[0, slot], lta.at[0, slot], slot, inner), cond)

    def lend_to(i, n, slot, to, cond):
        send(lambda: copy(lend.at[n], lta.at[0, slot], ls.at[9, i], lr.at[0, slot], to), cond)

    def give(kk):
        if kk < 2:

            @pl.when(home)
            def _():
                pass_on(slots[kk], home)

        if kk in (0, 2):

            @pl.when(helper)
            def _():
                lend_to(kk, kk // 2, (ri, 2)[kk // 2], outer, helper)

        @pl.when(home)
        def _():
            spread(kk, home)

    def take(kk, cond):
        @pl.when(cond)
        def _():
            slot = slots[kk]
            here = lta.at[0, slot]
            lcopy(0, here, here, slot, inner).wait_recv()
            spread(kk, cond)

    def yrelay(kk, cond):
        @pl.when(cond)
        def _():
            slot = slots[kk]
            low, high = lta.at[3, slot], lta.at[1, slot]
            lcopy(1, low.at[0], low.at[0], slot, yp).wait_recv()
            send(lambda: lcopy(3, lta.at[3, slot, 0], lta.at[2, slot, 0], slot, yp), cond)
            lcopy(2, high.at[1], high.at[1], slot, ym).wait_recv()
            send(lambda: lcopy(4, lta.at[1, slot, 1], lta.at[2, slot, 1], slot, ym), cond)
            lcopy(10, low.at[1], low.at[1], slot, yp).wait_recv()
            send(lambda: lcopy(8, lta.at[3, slot], lta.at[3, slot], slot, mate), cond)
            lcopy(11, high.at[0], high.at[0], slot, ym).wait_recv()
            send(lambda: lcopy(6, lta.at[1, slot], lta.at[1, slot], slot, mate), cond)

    def far(kk, cond):
        @pl.when(cond)
        def _():
            slot = slots[kk]
            one, two = lta.at[2, slot, 0], lta.at[2, slot, 1]
            lcopy(3, one, one, slot, yp).wait_recv()
            lcopy(4, two, two, slot, ym).wait_recv()
            send(lambda: lcopy(7, lta.at[2, slot], lta.at[2, slot], slot, mate), cond)

    def weights(n):
        if n == 0:
            wcopy(wz, 0, 0, 3, zp).wait_recv()
            wcopy(wz, 1, 0, 1, zm).wait_recv()
            send(lambda: wcopy(wz, 2, 3, 2, zp))
        elif n == 1:
            wcopy(wz, 2, 3, 2, zp).wait_recv()
            wx[0] = wz[0] + wz[1] + wz[2] + wz[3]
            send(lambda: wcopy(wx, 3, 0, 3, xp))
            send(lambda: wcopy(wx, 4, 0, 1, xm))
        elif n == 2:
            wcopy(wx, 3, 0, 3, xp).wait_recv()
            wcopy(wx, 4, 0, 1, xm).wait_recv()
            send(lambda: wcopy(wx, 5, 3, 2, xp))
        else:
            wcopy(wx, 5, 3, 2, xp).wait_recv()

    calls = {
        "s1a": s1a, "s1b": s1b, "s2a": s2a, "s2b": s2b, "s3": s3, "s4": s4, "kr": krelay, "w": weights,
        "o": lambda kk: take(kk, other), "yh": lambda kk: yrelay(kk, home), "yo": lambda kk: yrelay(kk, other),
        "rh": lambda kk: far(kk, home), "ro": lambda kk: far(kk, other),
    }

    def tri(n):
        return (n * (n + 1) // 2) % 4

    def project(kk):
        slot = (tri(kk) * ro) % 4
        both = vt[slot].reshape(2 * occ, mm)
        pts = lax.dot_general(both, coll[...], NT, preferred_element_type=F32).astype(BF16)
        for side in range(2):
            lb[slot, side] = pts[side * occ : (side + 1) * occ].T

        @pl.when(home)
        def _():
            lta[0, slot] = pts.reshape(2, occ, rows)

        @pl.when(jnp.logical_and(helper, kk % 2 == 0))
        def _():
            lend[kk // 2] = pts.reshape(2, occ, rows)

    def arrived(kk, jj):
        @pl.when(jnp.logical_not(lead))
        def _():
            slot = (tri(kk) * ro) % 4
            yr = (x + tri(jj) - y + 4) % 4
            here = lta.at[yr, slot]
            lcopy(5 + yr, here, here, slot, mate).wait_recv()

    def unit(kk, jj, part):
        slot = (tri(kk) * ro) % 4
        j = tri(jj)
        yr = (x + j - y + 4) % 4

        total = [None, None]
        for q in range(rows // TILE):
            cols = pl.ds(q * TILE, TILE)
            kq = kb[j, part, cols].astype(F32)
            for side in range(2):
                green = jnp.dot(
                    lb[slot, side, part], lta[yr, slot, 1 - side, :, cols], preferred_element_type=F32
                )
                had = (kq * green).astype(BF16)
                more = lax.dot_general(
                    had, lta[yr, slot, side, :, cols], NT, preferred_element_type=F32
                )
                total[side] = more if total[side] is None else total[side] + more
        for side in range(2):
            grad[slot, side, part] += total[1 - side]

    for slot in range(4):
        for side in range(2):
            grad[slot, side] = jnp.zeros(grad.shape[2:], F32)

    project(0)
    pl.semaphore_wait(barrier, len(peers))
    def wcopy(buf, i, src, dst, to):
        return copy(buf.at[src], buf.at[dst], ws.at[i], wr.at[i], to)

    send(lambda: wcopy(wz, 0, 0, 3, zp))
    send(lambda: wcopy(wz, 1, 0, 1, zm))

    def orbitals():
        send(lambda: vcopy(0, 0, ri, c, hf, outer))
        send(lambda: vcopy(1, 0, ri, c, ho, outer))

    def kernels():
        send(lambda: kcopy(0, 3, 0, xp))
        send(lambda: kcopy(1, 1, 1, xm))
        send(lambda: kcopy(2, 3, 1, xp))
        send(lambda: kcopy(3, 1, 0, xm))

    calls["v0"], calls["k0"], calls["g0"] = orbitals, kernels, lambda: give(0)
    first = set()

    def run(tokens, ahead, part, waits):
        steps = []
        for token in tokens:
            if token[0] not in ("P", "U", "H"):
                ahead = ahead + [token]
                continue
            ids = ()
            if token[0] != "P" and token[2] not in first:
                first.add(token[2])
                ids = ((), ((3, 1, 0, xm),), ((2, 3, 1, xp),), ((4, 2, 0, xp), (5, 2, 1, xm)))[token[2]]
            steps.append((token, ahead, ids))
            ahead = []
        mixed = any(token[0] == "P" for token, _, _ in steps)

        def step(t, carry):
            kk, jj, proj = t * 0, t * 0, t < 0
            for n, (token, todo, ids) in enumerate(steps):
                here = t == n
                kk = jnp.where(here, token[1], kk)
                if token[0] == "P":
                    proj = jnp.logical_or(proj, here)
                else:
                    jj = jnp.where(here, token[2], jj)
                if not todo and not ids and token[0] != "P":
                    continue

                @pl.when(here)
                def _():
                    for one in todo:
                        calls[one[0]](*one[1:])
                    if token[0] == "P":
                        vmate(token[1])
                    for one in ids:
                        kcopy(*one).wait_recv()

            def block():
                if waits:
                    arrived(kk, jj)
                unit(kk, jj, part)

            if not mixed:
                block()
                return carry

            @pl.when(proj)
            def _():
                project(kk)

            for n, (token, _, _) in enumerate(steps):
                if token[0] == "P":

                    @pl.when(t == n)
                    def _():
                        give(token[1])

            pl.when(jnp.logical_not(proj))(block)
            return carry

        lax.fori_loop(0, len(steps), step, 0)
        return ahead

    order = list(ORDER)
    lasts = [n for n, token in enumerate(order) if token[0] in ("P", "U")]
    cut = lasts[-1] + 1
    cuts = [n for n, token in enumerate(order) if token[0] == "H" and token[3] == 0]
    cut2 = cuts[-1] + 1
    cuts = [n for n, token in enumerate(order) if token[0] == "H"]
    cut3 = cuts[-1] + 1
    local.wait()
    rest = run(order[:cut], [], pl.ds(0, rows), True)

    weights(3)
    whole = wx[0] + wx[1] + wx[2] + wx[3]

    hrows = rows // 2
    qrows = rows // 4
    width = mm // 4
    piece = width // 4

    def xcopy(i, h, src, dst, to):
        return copy(src, dst, os_.at[i, h], or_.at[i, h], to)

    def acopy(h):
        return (
            xcopy(0, h, po.at[h, 0, pl.ds(0, qrows)], xa.at[h], xp),
            xcopy(1, h, po.at[h, 0, pl.ds(qrows, qrows)], xb.at[h], xm),
        )

    def bcopy(h):
        return xcopy(2, h, po.at[h, 1], xl.at[h], xp), xcopy(3, h, po.at[h, 2], xr.at[h], xm)

    def part_of(h):
        return pl.ds(pl.multiple_of(h * hrows, 16), hrows)

    def scale(h):
        def one(i, carry):
            slot, side = i // 2, i % 2
            share = (2.0 * wz[slot] / whole)[0:1, :occ]
            lb[slot, side, part_of(h)] = (grad[slot, side, part_of(h)] * share).astype(BF16)
            return carry

        lax.fori_loop(0, 8, one, 0)

    def term(h, d):
        cols = pl.ds(pl.multiple_of(((x + d) % 4) * width, 128), width)
        acc = None
        for slot in range(4):
            for side in range(2):
                one = jnp.dot(
                    lb[slot, side, part_of(h)], vt[slot, side, :, cols], preferred_element_type=F32
                )
                acc = one if acc is None else acc + one
        return acc

    def send_far(h):
        po[h, 0] = term(h, 2).astype(BF16)
        for one in acopy(h):
            one.start()

    def send_up(h):
        chunk[...] = term(h, 1)
        acopy(h)[0].wait_recv()
        po[h, 1, :qrows] = (chunk[:qrows] + xa[h].astype(F32)).astype(BF16)
        po[h, 1, qrows:] = chunk[qrows:].astype(BF16)
        bcopy(h)[0].start()

    def send_down(h):
        chunk[...] = term(h, 3)
        acopy(h)[1].wait_recv()
        po[h, 2, :qrows] = chunk[:qrows].astype(BF16)
        po[h, 2, qrows:] = (chunk[qrows:] + xb[h].astype(F32)).astype(BF16)
        bcopy(h)[1].start()

    def keep_own(h):
        own[h] = term(h, 0)

    low = piece // 2

    def zrows(d, n, size):
        return pl.ds(pl.multiple_of(((zh + d) % 4) * piece + n, 16), size)

    def zcopies(h):
        return (
            xcopy(4, h, zs.at[h, 0], za.at[h], zp),
            xcopy(5, h, zs.at[h, 1], zb.at[h], zm),
            xcopy(6, h, zt.at[h, 0], zl_.at[h], zp),
            xcopy(7, h, zt.at[h, 1], zr_.at[h], zm),
        )

    def gather(h):
        for one in bcopy(h):
            one.wait_recv()
        tz[h] = (own[h] + xl[h].astype(F32) + xr[h].astype(F32)).T
        zs[h, 0] = tz[h, zrows(2, 0, low)].astype(BF16)
        zs[h, 1] = tz[h, zrows(2, low, low)].astype(BF16)
        for one in zcopies(h)[:2]:
            one.start()

    def turn(h):
        first, second, third, fourth = zcopies(h)
        first.wait_recv()
        zt[h, 0, :low] = (tz[h, zrows(1, 0, low)] + za[h].astype(F32)).astype(BF16)
        zt[h, 0, low:] = tz[h, zrows(1, low, low)].astype(BF16)
        third.start()
        second.wait_recv()
        zt[h, 1, :low] = tz[h, zrows(3, 0, low)].astype(BF16)
        zt[h, 1, low:] = (tz[h, zrows(3, low, low)] + zb[h].astype(F32)).astype(BF16)
        fourth.start()

    def finish(h):
        for one in zcopies(h)[2:]:
            one.wait_recv()
        out[:, h * hrows : (h + 1) * hrows] = (
            tz[h, zrows(0, 0, piece)] + zl_[h].astype(F32) + zr_[h].astype(F32)
        )

    def far_first(h):
        scale(h)
        send_far(h)

    calls.update(SF=far_first, SU=send_up, SD=send_down, KO=keep_own, G=gather, T=turn, F=finish)
    rest = run(order[cut:cut2], rest, pl.ds(0, hrows), True)
    rest = run(order[cut2:cut3], rest, pl.ds(hrows, hrows), False)
    for one in rest + order[cut3:]:
        calls[one[0]](*one[1:])

    for make, cond in sent:
        if cond is None:
            make().wait_send()
        else:
            pl.when(cond)(lambda: make().wait_send())
    for h in range(2):
        for one in acopy(h) + bcopy(h) + zcopies(h):
            one.wait_send()


def on_device(bra, ket, coll, kern, weight, group, occupied):
    bra_t, ket_t = bra[0].T, ket[0].T
    occ, mm = bra_t.shape
    rows = coll.shape[0]
    hrows, qrows, width = rows // 2, rows // 4, mm // 4
    piece = width // 4
    vmem = pl.BlockSpec(memory_space=pltpu.VMEM)
    smem = pl.BlockSpec(memory_space=pltpu.SMEM)
    dma = pltpu.SemaphoreType.DMA
    result = pl.pallas_call(
        kernel,
        out_shape=jax.ShapeDtypeStruct((piece, rows), F32),
        in_specs=[smem, smem, smem, vmem, vmem, vmem, pl.BlockSpec(memory_space=pl.ANY)],
        out_specs=vmem,
        scratch_shapes=[
            pltpu.VMEM((4, 2, occ, mm), BF16),
            pltpu.VMEM((4, 4, 2, occ, rows), BF16),
            pltpu.VMEM((4, 2, rows, occ), BF16),
            pltpu.VMEM((4, rows, rows), BF16),
            pltpu.VMEM((4, 2, rows, occ), F32),
            pltpu.VMEM((2, 2, occ, rows), BF16),
            pltpu.VMEM((4, 8, 256), F32),
            pltpu.VMEM((4, 8, 256), F32),
            pltpu.VMEM((hrows, width), F32),
            pltpu.VMEM((2, 3, hrows, width), BF16),
            pltpu.VMEM((2, qrows, width), BF16),
            pltpu.VMEM((2, qrows, width), BF16),
            pltpu.VMEM((2, hrows, width), BF16),
            pltpu.VMEM((2, hrows, width), BF16),
            pltpu.VMEM((2, hrows, width), F32),
            pltpu.VMEM((2, width, hrows), F32),
            pltpu.VMEM((2, 2, piece // 2, hrows), BF16),
            pltpu.VMEM((2, 2, piece, hrows), BF16),
            pltpu.VMEM((2, piece // 2, hrows), BF16),
            pltpu.VMEM((2, piece // 2, hrows), BF16),
            pltpu.VMEM((2, piece, hrows), BF16),
            pltpu.VMEM((2, piece, hrows), BF16),
            dma((12,)), dma((12,)), dma((12, 4)), dma((12, 4)), dma((6,)), dma((6,)),
            dma((6,)), dma((6,)), dma((8, 2)), dma((8, 2)), dma,
        ],
        compiler_params=pltpu.CompilerParams(
            collective_id=0, has_side_effects=True, vmem_limit_bytes=67043328
        ),
    )(weight, group, occupied, bra_t, ket_t, coll, kern)
    return result.T


def solution(mesh):
    in_specs = (
        P("walk", None, None),
        P("walk", None, None),
        P("pt", None),
        P("pt", "walk"),
        P("walk"),
        P("walk"),
        P(),
    )
    return jax.shard_map(
        on_device, mesh=mesh, in_specs=in_specs, out_specs=P("pt", "walk"), check_vma=False
    )
```
